32 devices in a mesh: beam: 2 (over y), chan: 4 (over z), tgrp: 2 (over x), pol: 2 (over core).
Axes of the slice: x: 2, y: 2, z: 4, core: 2. Of those that a mesh axis runs over, the one named last changes fastest.
Arguments:
- voltages: bfloat16 [16, 8192, 512], P(('beam', 'chan', 'tgrp'), None, 'pol'), parts along dimension 0, may hold values from -6 to 6
- filter_taps: float32 [4, 8192], replicated, may hold values from -0.03125 to 0.03125
Outputs:
- visibility: float32 [512, 16, 2, 512], P('tgrp', ('beam', 'chan'), None, 'pol'), parts along dimension 1
The draws below stay inside these ranges and needn't reach their ends.
There are 2 independent parts, one for each index of `beam`. The reference program is written for one: setup_inputs(seed, part) draws one part's arguments, and reference() takes and returns one part's arrays. A program takes and returns all parts, laid end to end along the dimension named above; an argument that names none is the same for every part. Nothing has to cross between parts.
All inputs are finite; a program needn't handle non-finite values.
Results may differ from the reference program's by a relative error of at most 0.013.
Values may be sent and summed in bfloat16 or wider, within the bound.
A program may use at most 64 MiB of HBM per device.

```python
import jax
import jax.numpy as jnp
from jax import lax

LEN = 8192
INPUTS = 512
TAPS = 4
BAND_START = 1024
BAND = 8
FRAMES = 8


def block_scale(own_key, shape, cuts, least, largest):
    def one(position, shards_of):
        draws = jax.random.uniform(jax.random.fold_in(jax.random.fold_in(own_key, 6), position), (shards_of,), jnp.float32, least / len(cuts), largest / len(cuts))
        return jnp.repeat(jnp.exp(draws), shape[position] // shards_of).reshape((-1,) + (1,) * (len(shape) - position - 1))

    gain = one(*cuts[0])
    for cut in cuts[1:]:
        gain = gain * one(*cut)
    return gain


def centred(key, dims, width, bound, shards=(), held_as=jnp.bfloat16):
    result = width * jax.random.normal(key, dims, jnp.float32)
    if shards:
        result = result * block_scale(key, dims, shards, -0.22, 0.18)
    return jnp.clip(result, -bound, bound).astype(held_as)


def setup_inputs(seed: int = 0, part: int = 0) -> dict:
    key_of = jax.random.split(jax.random.key(seed), 3)
    part_splits = jax.random.split(jax.random.fold_in(key_of[2], part), 3)
    return {
        "voltages": centred(part_splits[0], (FRAMES, LEN, INPUTS), 1.0, 6.0, ((0, 8), (2, 2))),
        "filter_taps": centred(key_of[1], (TAPS, LEN), (TAPS * LEN) ** -0.5, 0.03125, (), jnp.float32),
    }


def reference(voltages, filter_taps):
    frames, length, inputs = voltages.shape
    lead_count = TAPS - 1

    def one_frame(frame_index):
        windowed = jnp.zeros((length, inputs), jnp.float32)
        for tap_index in range(TAPS):
            source = frame_index - lead_count + tap_index
            picked = lax.dynamic_index_in_dim(voltages, jnp.maximum(source, 0).astype(jnp.int32), 0, keepdims=False)
            weight = jnp.where(source >= 0, 1.0, 0.0).astype(jnp.float32)
            windowed = windowed + weight * filter_taps[tap_index][:, None] * picked.astype(jnp.float32)
        spectrum = jnp.fft.rfft(windowed, axis=0)[BAND_START:BAND_START + BAND]
        return jnp.stack([jnp.real(spectrum), jnp.imag(spectrum)], 0).astype(jnp.bfloat16)

    spectra = lax.map(one_frame, jnp.arange(frames, dtype=jnp.int32))
    wide_spectra = spectra.astype(jnp.float32)
    real_part = jnp.einsum("frki,frkj->ikj", wide_spectra, wide_spectra)
    imag_part = jnp.einsum("fki,fkj->ikj", wide_spectra[:, 1], wide_spectra[:, 0]) - jnp.einsum("fki,fkj->ikj", wide_spectra[:, 0], wide_spectra[:, 1])
    return jnp.stack([real_part, imag_part], 2) * (1.0 / FRAMES)
```

```python
import functools
import math

import jax
import jax.numpy as jnp
import numpy as np
from jax import lax
from jax.experimental import pallas as pl
from jax.experimental.pallas import tpu as pltpu
from jax.sharding import PartitionSpec as P

BAND_START = 1024
CH_DEV = 2
CHUNKS = 8
NEAR = 512
TILE = 256
VMEM_BYTES = 64 * 2**20
SPARE_BYTES = 72 * 2**10
LINK = jnp.bfloat16
MESH = pl.DeviceIdType.MESH


def twiddle_table(length, chans):
    axes = (np.arange(chans), np.arange(4 // CH_DEV), np.arange(2), np.arange(CH_DEV))
    block, _, part, sub = np.meshgrid(*axes, indexing="ij")
    channel = (BAND_START + block * CH_DEV + sub).reshape(-1, 1)
    angles = (channel * np.arange(length)[None] % length) * (2.0 * math.pi / length)
    is_real = part.reshape(-1, 1) == 0
    near, turn = angles[:, :NEAR], angles[:, ::NEAR]
    rows, turns = turn.shape
    table = np.zeros((2 * rows, NEAR + -(-turns // 128) * 128), np.float32)
    table[:rows, :NEAR] = np.where(is_real, np.cos(near), -np.sin(near))
    table[rows:, :NEAR] = np.where(is_real, -np.sin(near), np.cos(near))
    table[:rows, NEAR : NEAR + turns] = np.cos(turn)
    table[rows:, NEAR : NEAR + turns] = np.where(is_real, np.sin(turn), -np.sin(turn))
    return table


def tap_sum_matrix(frames, taps, swapped):
    rows, cols = CH_DEV * frames * 2, frames * taps * 2 * CH_DEV
    row = lax.broadcasted_iota(jnp.int32, (rows, cols), 0)
    col = lax.broadcasted_iota(jnp.int32, (rows, cols), 1)
    row_sub, row_frame, row_part = row // (2 * frames), row // 2 % frames, row % 2
    col_frame, col_tap = col // (taps * 2 * CH_DEV), col // (2 * CH_DEV) % taps
    col_part, col_sub = col // CH_DEV % 2, col % CH_DEV
    hit = (row_sub == col_sub) & (row_frame == col_frame + col_tap)
    if swapped:
        hit = hit & (row_part != col_part)
        value = jnp.where(row_part == 0, 1.0, -1.0)
    else:
        hit = hit & (row_part == col_part)
        value = jnp.float32(1.0)
    return jnp.where(hit, value, 0.0).astype(jnp.bfloat16)


def tap_summed(matrix, slots):
    flat = slots.reshape(slots.shape[0] * slots.shape[1], slots.shape[2])
    high = flat.astype(jnp.bfloat16)
    total = jnp.dot(matrix, high, preferred_element_type=jnp.float32)
    if flat.dtype == jnp.float32:
        low = (flat - high.astype(jnp.float32)).astype(jnp.bfloat16)
        total = total + jnp.dot(matrix, low, preferred_element_type=jnp.float32)
    return total.astype(jnp.bfloat16)


def power_kernel(row_terms, col_terms, out_hbm, out_ref, wide_ref, sems):
    frames, slot, half = col_terms.shape
    taps = slot // (2 * CH_DEV)
    matrix = tap_sum_matrix(frames, taps, False)
    both = jnp.concatenate([matrix, tap_sum_matrix(frames, taps, True)], 0)
    col_side = tap_summed(matrix, col_terms[...])
    row_side = tap_summed(both, row_terms[...])
    band = matrix.shape[0]
    rows = out_ref.shape[0] * 128 // (CH_DEV * 2 * half)
    tiles = half // 128
    stride = CH_DEV * 2 * tiles
    pieces = rows // 64 if rows == half else 1
    size = rows // pieces
    writes = []
    for piece in range(pieces):
        for part in range(2):
            for sub in range(CH_DEV):
                span = slice(sub * 2 * frames, (sub + 1) * 2 * frames)
                row_span = slice(part * band + span.start, part * band + span.stop)
                lanes = slice(piece * size, (piece + 1) * size) if rows == half else slice(None)
                vis = lax.dot_general(
                    row_side[row_span, lanes],
                    col_side[span],
                    (((0,), (0,)), ((), ())),
                    preferred_element_type=jnp.float32,
                ) * (1.0 / frames)
                if rows != half:
                    wide_ref[...] = vis
                    first = lax.axis_index("tgrp") * rows % half
                    vis = wide_ref[pl.ds(pl.multiple_of(first, 8), rows), :]
                for tile in range(tiles):
                    start = piece * size * stride + sub * 2 * tiles + tile * 2 + part
                    out_ref[pl.ds(start, size, stride=stride), :] = vis[:, tile * 128 : (tile + 1) * 128]
        region = pl.ds(piece * size * stride, size * stride)
        writes.append(pltpu.make_async_copy(out_ref.at[region], out_hbm.at[region], sems.at[piece]))
        writes[-1].start()
    for write in writes:
        write.wait()


def exchange_kernel(
    chans, groups, volt_hbm, taps_hbm, tw_hbm, row_terms, col_terms,
    volt, taps, tw, weights, sent, cols, rows, load_sem, col_send, row_send, col_recv, row_recv, ready,
):
    length, half = volt.shape
    tap_count = taps.shape[0]
    frames = chans * groups
    me_c, me_g, me_p = lax.axis_index("chan"), lax.axis_index("tgrp"), lax.axis_index("pol")
    me_f = me_c * groups + me_g
    me = me_f * 2 + me_p
    per_half = groups // 2
    my_half = me_g // per_half
    chunk = length // CHUNKS
    per_block = 2 * CH_DEV
    near = tap_count // 2
    late = frames - near

    def device(frame, pol):
        return {"chan": frame // groups, "tgrp": lax.rem(frame, groups), "pol": pol}

    loads = [
        pltpu.make_async_copy(taps_hbm, taps, load_sem.at[0]),
        pltpu.make_async_copy(tw_hbm, tw, load_sem.at[1]),
    ]
    for step in range(CHUNKS):
        span = pl.ds(step * chunk, chunk)
        loads.append(pltpu.make_async_copy(volt_hbm.at[0, span], volt.at[span], load_sem.at[2 + step]))
    for load in loads:
        load.start()

    barrier = pltpu.get_barrier_semaphore()

    @pl.loop(me + 1, frames * 2)
    def _(other):
        pl.semaphore_signal(barrier, inc=1, device_id=device(other // 2, lax.rem(other, 2)), device_id_type=MESH)

    pl.when(me > 0)(lambda: pl.semaphore_wait(barrier, me))
    takes_rows = my_half != me_p

    @pl.loop(0, me_f)
    def _(frame):
        pl.semaphore_signal(ready.at[me], inc=1, device_id=device(frame, me_p), device_id_type=MESH)

        @pl.when(takes_rows)
        def _():
            pl.semaphore_signal(ready.at[me], inc=1, device_id=device(frame, 1 - me_p), device_id_type=MESH)

    @pl.when(takes_rows & (me_p == 1))
    def _():
        pl.semaphore_signal(ready.at[me], inc=1, device_id=device(me_f, 1 - me_p), device_id_type=MESH)

    for slots in (cols, rows):
        slots[late:, near * per_block :, :] = jnp.zeros((near, (tap_count - near) * per_block, half), LINK)
    loads[0].wait()
    loads[1].wait()
    table_rows = tw.shape[0] // 2

    def compute(live):
        pairs = live * per_block // 8
        terms = pairs * table_rows
        own, other = tw[:table_rows, :NEAR], tw[table_rows:, :NEAR]
        first = lax.broadcasted_iota(jnp.int32, (8, NEAR), 0) < per_block
        for turn in range(length // NEAR):
            span = slice(turn * NEAR, (turn + 1) * NEAR)
            column = slice(NEAR + turn, NEAR + turn + 1)
            table = tw[:table_rows, column] * own + tw[table_rows:, column] * other
            gains = []
            for pair in range(pairs):
                t = tap_count - 1 - 2 * pair
                gains.append(
                    jnp.where(
                        first,
                        jnp.broadcast_to(taps[t : t + 1, span], (8, NEAR)),
                        jnp.broadcast_to(taps[t - 1 : t, span], (8, NEAR)),
                    )
                )
            wide = jnp.concatenate(
                [table[b * 8 : (b + 1) * 8] * gains[pair] for b in range(chans) for pair in range(pairs)], 0
            )
            high = wide.astype(jnp.bfloat16)
            weights[:terms, span] = high
            weights[terms : 2 * terms, span] = (wide - high.astype(jnp.float32)).astype(jnp.bfloat16)

        def multiply(*sums):
            for step in range(CHUNKS):
                loads[2 + step].wait()
                for tile in range(chunk // TILE):
                    place = step * (chunk // TILE) + tile
                    unit, stage = place % 2, place // 2 % 2
                    span = slice(place * TILE, (place + 1) * TILE)
                    pltpu.matmul_push_rhs(volt[span], stage, unit)
                    pltpu.matmul_acc_lhs(sums[unit], weights[: 2 * terms, span], load_staged_rhs=stage)
            return pltpu.matmul_pop(sums[0]) + pltpu.matmul_pop(sums[1])

        total = pl.run_scoped(
            multiply,
            pltpu.ACC(mxu_id=0)((2 * terms, half), jnp.float32),
            pltpu.ACC(mxu_id=1)((2 * terms, half), jnp.float32),
        )
        return (total[:terms] + total[terms:]).reshape(chans, live * per_block, half).astype(LINK)

    def col_copy(source, dest, live, index):
        span = pl.ds(0, live * per_block)
        return pltpu.make_async_remote_copy(
            src_ref=sent.at[dest // groups, span],
            dst_ref=cols.at[source, span],
            send_sem=col_send.at[index],
            recv_sem=col_recv.at[source],
            device_id=device(dest, me_p),
            device_id_type=MESH,
        )

    def row_copy(source, dest, live, index):
        span = pl.ds(0, live * per_block)
        return pltpu.make_async_remote_copy(
            src_ref=sent.at[dest // groups, span],
            dst_ref=rows.at[source, span],
            send_sem=row_send.at[index],
            recv_sem=row_recv.at[source],
            device_id=device(dest, 1 - me_p),
            device_id_type=MESH,
        )

    def feeds_rows(frame):
        return lax.rem(frame, groups) // per_half == me_p

    def start_all(live):
        def send_rows(frame, wait):
            @pl.when(feeds_rows(frame))
            def _():
                pl.when(wait)(lambda: pl.semaphore_wait(ready.at[frame * 2 + 1 - me_p], 1))
                row_copy(me_f, frame, live, frame).start()

        @pl.loop(0, me_f)
        def _(frame):
            col_copy(me_f, frame, live, frame).start()
            send_rows(frame, False)

        send_rows(me_f, me_p == 0)

        @pl.loop(me_f + 1, frames)
        def _(frame):
            pl.semaphore_wait(ready.at[frame * 2 + me_p], 1)
            col_copy(me_f, frame, live, frame).start()
            send_rows(frame, True)

    def wait_all(live):
        for frame in range(frames):
            pl.when(frame != me_f)(lambda: col_copy(me_f, frame, live, frame).wait_send())
            pl.when(feeds_rows(frame))(lambda: row_copy(me_f, frame, live, frame).wait_send())

    @pl.when(me_f < late)
    def _():
        sent[...] = compute(tap_count)
        start_all(tap_count)

    @pl.when(me_f >= late)
    def _():
        sent[:, : near * per_block, :] = compute(near)
        sent[:, near * per_block :, :] = jnp.zeros((chans, (tap_count - near) * per_block, half), LINK)
        start_all(near)

    cols[me_f] = sent[me_c]

    def live_of(source):
        return near if source >= late else tap_count

    def receive(sources):
        for source in sources:
            pl.when(source != me_f)(lambda: col_copy(source, me_f, live_of(source), 0).wait_recv())
            pl.when(takes_rows)(lambda: row_copy(source, me_f, live_of(source), 0).wait_recv())

    receive(range(late))
    pl.when(me_f < late)(lambda: wait_all(tap_count))
    pl.when(me_f >= late)(lambda: wait_all(near))
    receive(range(late, frames))

    col_terms[...] = cols[...]

    @pl.when(jnp.logical_not(takes_rows))
    def _():
        row_terms[...] = cols[...]

    @pl.when(takes_rows)
    def _():
        row_terms[...] = rows[...]


def body(voltages, filter_taps):
    chans, groups = lax.axis_size("chan"), lax.axis_size("tgrp")
    _, length, half = voltages.shape
    taps = filter_taps.shape[0]
    frames = chans * groups
    slot = taps * 2 * CH_DEV
    table = jnp.asarray(twiddle_table(length, chans))
    vmem = pl.BlockSpec(memory_space=pltpu.VMEM)
    row_terms, col_terms = pl.pallas_call(
        functools.partial(exchange_kernel, chans, groups),
        out_shape=(
            pltpu.VMEM((frames, slot, half), LINK),
            pltpu.VMEM((frames, slot, half), LINK),
        ),
        in_specs=[pl.BlockSpec(memory_space=pl.ANY)] * 3,
        out_specs=(vmem, vmem),
        scratch_shapes=[
            pltpu.VMEM((length, half), jnp.bfloat16),
            pltpu.VMEM(filter_taps.shape, jnp.float32),
            pltpu.VMEM(table.shape, jnp.float32),
            pltpu.VMEM((2 * chans * slot, length), jnp.bfloat16),
            pltpu.VMEM((chans, slot, half), LINK),
            pltpu.VMEM((frames, slot, half), LINK),
            pltpu.VMEM((frames, slot, half), LINK),
            pltpu.SemaphoreType.DMA((2 + CHUNKS,)),
            pltpu.SemaphoreType.DMA((frames,)),
            pltpu.SemaphoreType.DMA((frames,)),
            pltpu.SemaphoreType.DMA((frames,)),
            pltpu.SemaphoreType.DMA((frames,)),
            pltpu.SemaphoreType.REGULAR((frames * 2,)),
        ],
        compiler_params=pltpu.CompilerParams(collective_id=0, has_side_effects=True, vmem_limit_bytes=VMEM_BYTES - SPARE_BYTES - 4 * frames * slot * half),
        name="exchange",
    )(voltages, filter_taps, table)
    rows = half * lax.axis_size("pol") // groups
    tiles = half // 128
    powers = pl.pallas_call(
        power_kernel,
        out_shape=jax.ShapeDtypeStruct((rows * CH_DEV * tiles * 2, 128), jnp.float32),
        in_specs=[vmem, vmem],
        out_specs=pl.BlockSpec(memory_space=pltpu.HBM),
        scratch_shapes=[
            pltpu.VMEM((rows * CH_DEV * tiles * 2, 128), jnp.float32),
            pltpu.VMEM((half, half) if rows != half else (8, 128), jnp.float32),
            pltpu.SemaphoreType.DMA((max(1, rows // 64),)),
        ],
        compiler_params=pltpu.CompilerParams(vmem_limit_bytes=VMEM_BYTES // 4),
        name="powers",
    )(row_terms, col_terms)
    powers = powers.reshape(rows, CH_DEV, tiles, 2, 128).transpose(0, 1, 3, 2, 4)
    return powers.reshape(rows, CH_DEV, 2, half)


def solution(mesh):
    return jax.shard_map(
        body,
        mesh=mesh,
        in_specs=(P(("beam", "chan", "tgrp"), None, "pol"), P()),
        out_specs=P("tgrp", ("beam", "chan"), None, "pol"),
        check_vma=False,
    )
```
